32 devices in a mesh: batch: 4 (over y, x), seq: 2 (over core), tp: 4 (over z).
Axes of the slice: x: 2, y: 2, z: 4, core: 2. Of those that a mesh axis runs over, the one named last changes fastest.
Arguments:
- values: bfloat16 [8192, 8192], P(('batch', 'seq'), 'tp'), parts along dimension 0, may hold values from -6 to 6
- gate_in: bfloat16 [8192, 8192], P(('batch', 'seq'), 'tp'), parts along dimension 0, may hold values from -6 to 6
- write_proj: bfloat16 [8192, 1024], P(('batch', 'seq'), 'tp'), parts along dimension 0, may hold values from -0.59765625 to 0.59765625
- read_proj: bfloat16 [8192, 1024], P(('batch', 'seq'), 'tp'), parts along dimension 0, may hold values from -6 to 6
- step_size: float32 [8192, 64], P(('batch', 'seq'), 'tp'), parts along dimension 0, may hold values from 0.02 to 0.2
- log_gate: float32 [8192, 64], P(('batch', 'seq'), 'tp'), parts along dimension 0, may hold values from -4.5 to 0, as said below
- skip_gain: float32 [64], P('tp'), may hold values from 0.5 to 4
- norm_gain: bfloat16 [8192], P('tp'), may hold values from 0.5 to 1.5
- history: float32 [256, 128, 128], P(('batch', 'tp')), parts along dimension 0, may hold values from -6 to 6
Outputs:
- normed: bfloat16 [8192, 8192], P(('batch', 'seq'), 'tp'), parts along dimension 0
- final_state: float32 [256, 128, 128], P(('batch', 'tp'), 'seq'), parts along dimension 0
The draws below stay inside these ranges and needn't reach their ends.
There are 4 independent parts, one for each index of `batch`. The reference program is written for one: setup_inputs(seed, part) draws one part's arguments, and reference() takes and returns one part's arrays. A program takes and returns all parts, laid end to end along the dimension named above; an argument that names none is the same for every part. Nothing has to cross between parts.
Inputs may be any that keep to these rules, and one draw needn't show every extreme that they name: `log_gate`: negative everywhere.
All inputs are finite; a program needn't handle non-finite values.
Results may differ from the reference program's by a relative error of at most 0.001.
Values sent between devices are 32-bit elements; how exact they have to be, the bound alone decides.
A program may use at most 128 MiB of HBM per device.

```python
import math
import jax
import jax.numpy as jnp
from jax import lax

H = 64
P_SIZE = 128
N = 128
G = 8
TOKENS = 2048


def draw_log_gate(key, part):
    keys = jax.random.split(jax.random.fold_in(key, 17), 9)
    fast_share = 0.4
    fast_pick = jax.random.uniform(keys[0], (H,)) < fast_share
    slow_rate = jnp.exp(jax.random.uniform(keys[1], (H,), minval=math.log(0.1), maxval=math.log(0.5))) / TOKENS
    fast_rate = jnp.exp(jax.random.uniform(keys[2], (H,), minval=math.log(1.0 / 50.0), maxval=math.log(1.0 / 30.0)))
    channel_fading_speed = jnp.where(fast_pick, fast_rate, slow_rate)
    segment = jnp.exp(jax.random.uniform(keys[3], (16,), minval=math.log(0.5), maxval=math.log(1.5)))
    position = jnp.arange(TOKENS)
    interval_speed = segment[position * 16 // TOKENS]
    rough_guess = jax.random.uniform(keys[4], (TOKENS, H), minval=0.5, maxval=1.5)
    spots = jax.random.randint(keys[5], (3,), 0, TOKENS)
    stacked_levels = jnp.log(jax.random.uniform(keys[6], (3, H), minval=0.5, maxval=0.8))
    agreeing_tally = (position[:, None, None] == spots[None, :, None]).astype(jnp.float32)
    symbol_run_length = jnp.sum(agreeing_tally * stacked_levels[None], axis=1)
    rapid_head = jax.random.randint(keys[7], (), 0, H)
    rapid_rate = jax.random.uniform(keys[8], (), minval=1.2, maxval=1.4)
    common_amount = channel_fading_speed[None, :] * interval_speed[:, None] * rough_guess
    rapid_amount = rapid_rate * rough_guess
    rapid_column = (jnp.arange(H) == rapid_head)[None, :]
    decay_amount = jnp.where(rapid_column, rapid_amount, common_amount)
    return (symbol_run_length - decay_amount).astype(jnp.float32)


def levels(stream_key, extent, cuts, smallest, top_value):
    def one(dim, parts):
        draws = jax.random.uniform(jax.random.fold_in(jax.random.fold_in(stream_key, 6), dim), (parts,), jnp.float32, smallest / len(cuts), top_value / len(cuts))
        return jnp.repeat(jnp.exp(draws), extent[dim] // parts).reshape((-1,) + (1,) * (len(extent) - dim - 1))

    gain = one(*cuts[0])
    for cut in cuts[1:]:
        gain = gain * one(*cut)
    return gain


def centred(stream_key, dims, width, limit, cuts=(), held_as=jnp.bfloat16):
    factor_of = levels(stream_key, dims, cuts, -0.22, 0.18) if cuts else 1.0
    values = jax.random.normal(stream_key, dims, jnp.float32) * width * factor_of
    return jnp.minimum(jnp.maximum(values, -limit), limit).astype(held_as)


def setup_inputs(seed: int = 0, part: int = 0) -> dict:
    splits = jax.random.split(jax.random.key(seed), 10)
    part_splits = jax.random.split(jax.random.fold_in(splits[9], part), 10)
    values = centred(part_splits[0], (TOKENS, H * P_SIZE), 1.0, 6.0, ((0, 2), (1, 4)))
    gate_in = centred(part_splits[1], (TOKENS, H * P_SIZE), 1.0, 6.0, ((0, 2), (1, 4)))
    write_proj = centred(part_splits[2], (TOKENS, G * N), 0.1, 0.59765625, ((0, 2), (1, 4)))
    read_proj = centred(part_splits[3], (TOKENS, G * N), 1.0, 6.0, ((0, 2), (1, 4)))
    step_size = jnp.clip(0.02 + 0.18 * jax.random.uniform(part_splits[4], (TOKENS, H), jnp.float32) ** levels(part_splits[4], (TOKENS, H), ((0, 2), (1, 4)), -0.2, 0.2), 0.02, 0.2)
    log_gate = draw_log_gate(jax.random.fold_in(jax.random.fold_in(splits[9], part), 71), part)
    skip_gain = jnp.clip(jnp.exp(math.log(4.0) - 2.0794415 * jax.random.uniform(splits[6], (H,), jnp.float32) ** levels(splits[6], (H,), ((0, 4),), -0.2, 0.2)), 0.5, 4.0)
    norm_gain = jnp.clip(1.0 + 0.1 * jax.random.normal(splits[7], (H * P_SIZE,), jnp.float32), 0.5, 1.5).astype(jnp.bfloat16)
    history = centred(part_splits[8], (H, P_SIZE, N), 1.0, 6.0, ((0, 4),), jnp.float32)
    return {"values": values, "gate_in": gate_in, "write_proj": write_proj, "read_proj": read_proj, "step_size": step_size, "log_gate": log_gate, "skip_gain": skip_gain, "norm_gain": norm_gain, "history": history}


highest = lax.Precision.HIGHEST

def block_pass(state, inputs_blk, write_blk, read_blk, steps_blk, gates_blk):
    length = inputs_blk.shape[0]
    cumul = jnp.cumsum(gates_blk, axis=0)
    scores = jnp.einsum('tgn,sgn->gts', read_blk, write_blk, precision=highest)
    diffs = cumul[:, None] - cumul[None, :]
    causal = jnp.arange(length)[:, None] >= jnp.arange(length)[None, :]
    decay = jnp.exp(jnp.where(causal[:, :, None, None], diffs, -jnp.inf))
    weights = scores[:, None] * jnp.transpose(decay, (2, 3, 0, 1)) * jnp.transpose(steps_blk, (1, 2, 0))[:, :, None, :]
    inside = jnp.einsum('gkts,sgkp->tgkp', weights, inputs_blk, precision=highest)
    earlier = jnp.exp(cumul)[..., None] * jnp.einsum('gkpn,tgn->tgkp', state, read_blk, precision=highest)
    last_sum = cumul[-1]
    tail_weight = jnp.exp(last_sum[None] - cumul) * steps_blk
    new_state = jnp.exp(last_sum)[..., None, None] * state + jnp.einsum('sgk,sgkp,sgn->gkpn', tail_weight, inputs_blk, write_blk, precision=highest)
    return (new_state, inside + earlier, cumul)

def reference(values, gate_in, write_proj, read_proj, step_size, log_gate, skip_gain, norm_gain, history):
    per_group = H // G
    block = math.gcd(TOKENS, 256)
    blocks = TOKENS // block
    inputs_all = values.astype(jnp.float32).reshape(blocks, block, G, per_group, P_SIZE)
    write_all = write_proj.astype(jnp.float32).reshape(blocks, block, G, N)
    read_all = read_proj.astype(jnp.float32).reshape(blocks, block, G, N)
    steps_all = step_size.reshape(blocks, block, G, per_group)
    gates_all = log_gate.reshape(blocks, block, G, per_group)

    def advance(state, pieces):
        new_state, output_blk, cumul = block_pass(state, *pieces)
        return (new_state, output_blk)
    start = history.reshape(G, per_group, P_SIZE, N)
    final, outputs = lax.scan(advance, start, (inputs_all, write_all, read_all, steps_all, gates_all))
    inputs_flat = values.astype(jnp.float32).reshape(TOKENS, G, per_group, P_SIZE)
    outputs = outputs.reshape(TOKENS, G, per_group, P_SIZE) + skip_gain.reshape(G, per_group)[None, :, :, None] * inputs_flat
    gated = outputs * jax.nn.silu(gate_in.astype(jnp.float32).reshape(TOKENS, G, per_group, P_SIZE))
    meansq = lax.optimization_barrier(jnp.mean(gated * gated, axis=(2, 3), keepdims=True))
    result = gated * lax.rsqrt(meansq + 1e-05) * norm_gain.astype(jnp.float32).reshape(1, G, per_group, P_SIZE)
    normed = result.reshape(TOKENS, H * P_SIZE).astype(jnp.bfloat16)
    return (normed, final.reshape(H, P_SIZE, N))
```

```python
import functools
import math

import jax
import jax.numpy as jnp
from jax import lax
from jax.experimental import pallas as pl
from jax.experimental.pallas import tpu as pltpu
from jax.sharding import PartitionSpec as P

HIGH = lax.Precision.HIGHEST
LOG2E = math.log2(math.e)
MESH = pl.DeviceIdType.MESH
F32 = jnp.float32
BF16 = jnp.bfloat16


def upper(size):
    rows = lax.broadcasted_iota(jnp.int32, (size, size), 0)
    cols = lax.broadcasted_iota(jnp.int32, (size, size), 1)
    return rows <= cols


def split(value):
    high = value.astype(BF16)
    low = (value - high.astype(F32)).astype(BF16)
    return high, low


def turned(array, matrix):
    return lax.dot_general(
        array, matrix, (((0,), (0,)), ((), ())), precision=HIGH, preferred_element_type=F32
    )


def rows_of(gates, steps):
    size = gates.shape[0]
    ones = upper(size).astype(F32)
    rows = lax.broadcasted_iota(jnp.int32, (size, size), 0)
    cols = lax.broadcasted_iota(jnp.int32, (size, size), 1)
    eye = (rows == cols).astype(F32)
    cumul = turned(gates * LOG2E, ones)
    shift = cumul - turned(jnp.log2(steps), eye)
    last = cumul[:, size - 1 : size]
    return shift, last


def chain_kernel(
    peers, x_ref, b_ref, step_ref, gate_ref, hist_ref, ent_ref, fin_ref,
    state, total, recv, send, full, fin_recv, send_sem, recv_sem, fin_send_sem, fin_recv_sem,
):
    group, blk = pl.program_id(0), pl.program_id(1)
    groups, blocks = pl.num_programs(0), pl.num_programs(1)
    count = recv.shape[0]
    me = lax.axis_index("seq")
    size = b_ref.shape[0]
    width = b_ref.shape[1]
    heads = hist_ref.shape[0]
    per_group = heads // count
    share = fin_ref.shape[1]

    @pl.when((group == 0) & (blk == 0))
    def _():
        barrier = pltpu.get_barrier_semaphore()
        for by in range(1, peers):
            other = lax.rem(me + by, peers)
            pl.semaphore_signal(barrier, inc=1, device_id={"seq": other}, device_id_type=MESH)
        pl.semaphore_wait(barrier, peers - 1)

    shift, last = rows_of(gate_ref[...], step_ref[...])
    tails = jnp.exp2(last - shift)
    decays = jnp.exp2(jnp.broadcast_to(last, (heads, width)))
    turned_b = jnp.transpose(b_ref[...].astype(F32))

    @pl.when(blk == 0)
    def _():
        state[...] = jnp.zeros_like(state)
        total[...] = jnp.zeros_like(total)

    total[...] += jnp.broadcast_to(last, (heads, width))

    def update(first):
        for k in range(per_group):
            h = first + k
            cols = slice(k * width, (k + 1) * width)
            high, low = split(turned_b * tails[h : h + 1, :])
            x = x_ref[:, cols]
            delta = jnp.dot(high, x, preferred_element_type=F32) + jnp.dot(
                low, x, preferred_element_type=F32
            )
            state[:, cols] = decays[h : h + 1, :] * state[:, cols] + delta

    def joined(k, h, entering):
        cols = slice(k * width, (k + 1) * width)
        return jnp.exp2(total[h : h + 1, :]) * entering + state[:, cols]

    def link(g):
        return pltpu.make_async_remote_copy(
            src_ref=send.at[g], dst_ref=recv.at[g],
            send_sem=send_sem.at[g], recv_sem=recv_sem.at[g],
            device_id={"seq": jnp.minimum(me + 1, peers - 1)}, device_id_type=MESH,
        )

    for g in range(count):

        @pl.when(group == g)
        def _(g=g):
            update(g * per_group)

            @pl.when(blk == blocks - 1)
            def _():
                for k in range(per_group):
                    h = g * per_group + k
                    cols = slice(k * width, (k + 1) * width)
                    send[g, :, cols] = state[:, cols]

            @pl.when((blk == blocks - 1) & (me == 0))
            def _():
                for k in range(per_group):
                    h = g * per_group + k
                    cols = slice(k * width, (k + 1) * width)
                    entering = jnp.transpose(hist_ref[h])
                    ent_ref[g, :, cols] = entering
                    send[g, :, cols] = joined(k, h, entering)
                link(g).start()

    @pl.when((group == groups - 1) & (blk == blocks - 1))
    def _():
        def to_peer(d):
            return pltpu.make_async_remote_copy(
                src_ref=full.at[d], dst_ref=fin_recv,
                send_sem=fin_send_sem.at[d], recv_sem=fin_recv_sem,
                device_id={"seq": d}, device_id_type=MESH,
            )

        @pl.when(me > 0)
        def _():
            for g in range(count):
                link(g).wait_recv()
                for k in range(per_group):
                    h = g * per_group + k
                    cols = slice(k * width, (k + 1) * width)
                    entering = recv[g, :, cols]
                    ent_ref[g, :, cols] = entering
                    send[g, :, cols] = jnp.exp2(total[h : h + 1, :]) * entering + send[g, :, cols]

                @pl.when(me < peers - 1)
                def _(g=g):
                    link(g).start()

        @pl.when(me == peers - 1)
        def _():
            for g in range(count):
                for k in range(per_group):
                    h = g * per_group + k
                    cols = slice(k * width, (k + 1) * width)
                    closing = jnp.transpose(send[g, :, cols])
                    for d in range(peers - 1):
                        full[d, h] = closing[d * share : (d + 1) * share]
                    fin_ref[h] = closing[(peers - 1) * share :]
            for d in range(peers - 1):
                to_peer(d).start()
            for d in range(peers - 1):
                to_peer(d).wait_send()

        @pl.when(me < peers - 1)
        def _():
            for g in range(count):
                link(g).wait_send()
            to_peer(0).wait_recv()
            fin_ref[...] = fin_recv[...]


def mix_kernel(
    x_ref, z_ref, b_ref, c_ref, step_ref, gate_ref, skip_ref, gain_ref, ent_ref, out_ref,
    state, parts, gated,
):
    groups, width, span = state.shape
    size = b_ref.shape[0]
    per_group = span // width
    heads = groups * per_group

    @pl.when(pl.program_id(0) == 0)
    def _():
        for g in range(groups):
            for k in range(per_group):
                cols = slice(k * width, (k + 1) * width)
                entering = ent_ref[g, :, cols]
                high, low = split(entering)
                state[g, :, cols] = entering
                parts[g, :width, cols] = high
                parts[g, width:, cols] = low

    gates, steps = gate_ref[...], step_ref[...]
    shift, last = rows_of(gates, steps)
    tails = jnp.exp2(last - shift)
    decays = jnp.exp2(jnp.broadcast_to(last, (heads, width)))
    rows = lax.broadcasted_iota(jnp.int32, (size, size), 0)
    cols_at = lax.broadcasted_iota(jnp.int32, (size, size), 1)
    causal = rows >= cols_at
    cumul = jnp.dot(
        causal.astype(F32), gates * LOG2E, precision=HIGH, preferred_element_type=F32
    )
    for g in range(groups):
        write = b_ref[:, g * width : (g + 1) * width]
        read = c_ref[:, g * width : (g + 1) * width]
        scores = lax.dot_general(
            read, write, (((1,), (1,)), ((), ())), preferred_element_type=F32
        )
        scores = jnp.where(causal, scores, 0.0)
        turned_b = jnp.transpose(write.astype(F32))
        earlier = jnp.dot(
            jnp.concatenate([read, read], axis=1), parts[g], preferred_element_type=F32
        )
        squares = jnp.zeros((size, width), F32)
        for k in range(per_group):
            h = g * per_group + k
            cols = slice(k * width, (k + 1) * width)
            wide = slice(h * width, (h + 1) * width)
            x = x_ref[:, wide]
            along = jnp.broadcast_to(cumul[:, h : h + 1], (size, width))
            weights = scores * jnp.exp2(
                jnp.minimum(jnp.broadcast_to(cumul[:, h : h + 1], (size, size)) - shift[h : h + 1, :], 0.0)
            )
            left = jnp.concatenate(
                [
                    jnp.concatenate(split(weights), axis=1),
                    jnp.concatenate(split(turned_b * tails[h : h + 1, :]), axis=1),
                ],
                axis=0,
            )
            both = jnp.dot(left, jnp.concatenate([x, x], axis=0), preferred_element_type=F32)
            later = decays[h : h + 1, :] * state[g, :, cols] + both[size:]
            high, low = split(later)
            state[g, :, cols] = later
            parts[g, :width, cols] = high
            parts[g, width:, cols] = low
            y = both[:size] + jnp.exp2(along) * earlier[:, cols] + skip_ref[h] * x.astype(F32)
            z = z_ref[:, wide].astype(F32)
            value = y * (0.5 * z * (1.0 + jnp.tanh(0.5 * z)))
            gated[:, cols] = value
            squares = squares + value * value
        mean = jnp.sum(squares, axis=1, keepdims=True) * (1.0 / span)
        scale = jnp.broadcast_to(lax.rsqrt(mean + 1e-05), (size, width))
        for k in range(per_group):
            h = g * per_group + k
            cols = slice(k * width, (k + 1) * width)
            wide = slice(h * width, (h + 1) * width)
            out_ref[:, wide] = (
                gated[:, cols] * scale * gain_ref[:, wide].astype(F32)
            ).astype(BF16)


def body(
    values, gate_in, write_proj, read_proj, step_size, log_gate, skip_gain, norm_gain, history
):
    heads, head_size, width = history.shape
    groups = write_proj.shape[1] // width
    per_group = heads // groups
    span = per_group * head_size
    rows = values.shape[0]
    peers = lax.axis_size("seq")
    share = head_size // peers
    big = math.gcd(rows, 256)
    small = math.gcd(rows, 128)

    entering, final_state = pl.pallas_call(
        functools.partial(chain_kernel, peers),
        grid=(groups, rows // big),
        in_specs=[
            pl.BlockSpec((big, span), lambda g, c: (c, g)),
            pl.BlockSpec((big, width), lambda g, c: (c, g)),
            pl.BlockSpec((big, heads), lambda g, c: (c, 0)),
            pl.BlockSpec((big, heads), lambda g, c: (c, 0)),
            pl.BlockSpec((heads, head_size, width), lambda g, c: (0, 0, 0)),
        ],
        out_specs=[
            pl.BlockSpec((groups, width, span), lambda g, c: (0, 0, 0)),
            pl.BlockSpec((heads, share, width), lambda g, c: (0, 0, 0)),
        ],
        out_shape=[
            jax.ShapeDtypeStruct((groups, width, span), F32),
            jax.ShapeDtypeStruct((heads, share, width), F32),
        ],
        scratch_shapes=[
            pltpu.VMEM((width, span), F32),
            pltpu.VMEM((heads, width), F32),
            pltpu.VMEM((groups, width, span), F32),
            pltpu.VMEM((groups, width, span), F32),
            pltpu.VMEM((peers - 1, heads, share, width), F32),
            pltpu.VMEM((heads, share, width), F32),
            pltpu.SemaphoreType.DMA((groups,)),
            pltpu.SemaphoreType.DMA((groups,)),
            pltpu.SemaphoreType.DMA((peers - 1,)),
            pltpu.SemaphoreType.DMA,
        ],
        compiler_params=pltpu.CompilerParams(
            collective_id=0, has_side_effects=True, vmem_limit_bytes=40 << 20
        ),
        name="chain",
    )(values, write_proj, step_size, log_gate, history)

    normed = pl.pallas_call(
        mix_kernel,
        grid=(rows // small,),
        in_specs=[
            pl.BlockSpec((small, heads * head_size), lambda c: (c, 0)),
            pl.BlockSpec((small, heads * head_size), lambda c: (c, 0)),
            pl.BlockSpec((small, groups * width), lambda c: (c, 0)),
            pl.BlockSpec((small, groups * width), lambda c: (c, 0)),
            pl.BlockSpec((small, heads), lambda c: (c, 0)),
            pl.BlockSpec((small, heads), lambda c: (c, 0)),
            pl.BlockSpec(memory_space=pltpu.SMEM),
            pl.BlockSpec((1, heads * head_size), lambda c: (0, 0)),
            pl.BlockSpec((groups, width, span), lambda c: (0, 0, 0)),
        ],
        out_specs=pl.BlockSpec((small, heads * head_size), lambda c: (c, 0)),
        out_shape=jax.ShapeDtypeStruct((rows, heads * head_size), BF16),
        scratch_shapes=[
            pltpu.VMEM((groups, width, span), F32),
            pltpu.VMEM((groups, 2 * width, span), BF16),
            pltpu.VMEM((small, span), F32),
        ],
        compiler_params=pltpu.CompilerParams(vmem_limit_bytes=40 << 20),
        name="mix",
    )(
        values, gate_in, write_proj, read_proj, step_size, log_gate, skip_gain,
        norm_gain.reshape(1, -1), entering,
    )
    return normed, final_state


def solution(mesh):
    rows = P(("batch", "seq"), "tp")
    return jax.shard_map(
        body,
        mesh=mesh,
        in_specs=(rows, rows, rows, rows, rows, rows, P("tp"), P("tp"), P(("batch", "tp"), None, None)),
        out_specs=(rows, P(("batch", "tp"), "seq", None)),
        check_vma=False,
    )
```

```python
import functools
import math

import jax
import jax.numpy as jnp
from jax import lax
from jax.experimental import pallas as pl
from jax.experimental.pallas import tpu as pltpu
from jax.sharding import PartitionSpec as P

VMEM = 60 << 20
LOG2E = math.log2(math.e)
MESH = pl.DeviceIdType.MESH
F32 = jnp.float32
BF16 = jnp.bfloat16


def upper(size):
    rows = lax.broadcasted_iota(jnp.int32, (size, size), 0)
    cols = lax.broadcasted_iota(jnp.int32, (size, size), 1)
    return rows <= cols


def split(value):
    high = value.astype(BF16)
    low = (value - high.astype(F32)).astype(BF16)
    return high, low


def prefix_sums(rows):
    size = rows.shape[1]
    first = rows.astype(BF16)
    rest = rows - first.astype(F32)
    second = rest.astype(BF16)
    third = (rest - second.astype(F32)).astype(BF16)
    ones = upper(size).astype(BF16)
    return jnp.dot(
        jnp.concatenate([first, second, third], axis=1),
        jnp.concatenate([ones, ones, ones], axis=0),
        preferred_element_type=F32,
    )


def chain_kernel(
    peers, x_ref, b_ref, step_ref, gate_ref, hist_ref,
    ent_ref, fin_ref, shift_ref, last_ref, cols_ref,
    state, total, tails, recv, send, full, fin_recv,
    send_sem, recv_sem, fin_send_sem, fin_recv_sem,
):
    group, part = pl.program_id(0), pl.program_id(1)
    count, width, span = recv.shape
    blocks, heads, size = shift_ref.shape
    parts = b_ref.shape[0] // size
    steps = blocks // parts
    me = lax.axis_index("seq")
    per_group = heads // count
    share = fin_ref.shape[1]

    def peer(d):
        return dict(device_id={"seq": d}, device_id_type=MESH)

    @pl.when((group == 0) & (part == 0))
    def _():
        barrier = pltpu.get_barrier_semaphore()
        for by in range(1, peers):
            pl.semaphore_signal(barrier, inc=1, **peer(lax.rem(me + by, peers)))
        rows = [gate_ref[:, c * size : (c + 1) * size] for c in range(blocks)]
        cumul = prefix_sums(jnp.concatenate(rows, axis=0) * LOG2E)
        columns = jnp.transpose(cumul)
        after = jnp.zeros((heads, width), F32)
        for c in reversed(range(blocks)):
            here = cumul[c * heads : (c + 1) * heads]
            shift = here - jnp.log2(step_ref[:, c * size : (c + 1) * size])
            last = jnp.broadcast_to(here[:, size - 1 : size], (heads, width))
            shift_ref[c] = shift
            last_ref[c] = last
            cols_ref[c] = columns[:, c * heads : (c + 1) * heads]
            after = after + last
            tails[c] = jnp.exp2(after - shift)
        total[...] = jnp.exp2(after)

    turned_b = jnp.transpose(b_ref[...].astype(F32))

    def link(g):
        return pltpu.make_async_remote_copy(
            src_ref=send.at[g], dst_ref=recv.at[g],
            send_sem=send_sem.at[g], recv_sem=recv_sem.at[g],
            **peer(jnp.minimum(me + 1, peers - 1)),
        )

    def to_peer(d, g):
        return pltpu.make_async_remote_copy(
            src_ref=full.at[d, g], dst_ref=fin_recv.at[g],
            send_sem=fin_send_sem.at[d, g], recv_sem=fin_recv_sem.at[g],
            **peer(d),
        )

    for g in range(count):

        @pl.when(group == g)
        def _(g=g):
            @pl.when(part == 0)
            def _():
                state[g] = jnp.zeros((width, span), F32)

            for k in range(per_group):
                h = g * per_group + k
                cols = slice(k * width, (k + 1) * width)
                tail = jnp.concatenate(
                    [tails[part * parts + j, h : h + 1, :] for j in range(parts)], axis=1
                )
                left = jnp.concatenate(split(turned_b * tail), axis=0)
                both = jnp.dot(left, x_ref[:, cols], preferred_element_type=F32)
                state[g, :, cols] += both[:width] + both[width:]

            @pl.when(part == steps - 1)
            def _():
                if g == 0:
                    pl.semaphore_wait(pltpu.get_barrier_semaphore(), peers - 1)

                @pl.when(me == 0)
                def _():
                    for k in range(per_group):
                        h = g * per_group + k
                        cols = slice(k * width, (k + 1) * width)
                        entering = jnp.transpose(hist_ref[h])
                        ent_ref[g, :, cols] = entering
                        send[g, :, cols] = total[h : h + 1, :] * entering + state[g, :, cols]
                    link(g).start()

    @pl.when((group == count - 1) & (part == steps - 1))
    def _():
        @pl.when(me > 0)
        def _():
            for g in range(count):
                link(g).wait_recv()
                for k in range(per_group):
                    h = g * per_group + k
                    cols = slice(k * width, (k + 1) * width)
                    entering = recv[g, :, cols]
                    ent_ref[g, :, cols] = entering
                    send[g, :, cols] = total[h : h + 1, :] * entering + state[g, :, cols]

                @pl.when(me < peers - 1)
                def _(g=g):
                    link(g).start()

                @pl.when(me == peers - 1)
                def _(g=g):
                    for k in range(per_group):
                        cols = slice(k * width, (k + 1) * width)
                        closing = jnp.transpose(send[g, :, cols])
                        for d in range(peers - 1):
                            full[d, g, k] = closing[d * share : (d + 1) * share]
                        fin_ref[g * per_group + k] = closing[(peers - 1) * share :]
                    for d in range(peers - 1):
                        to_peer(d, g).start()

        @pl.when(me == peers - 1)
        def _():
            for g in range(count):
                for d in range(peers - 1):
                    to_peer(d, g).wait_send()

        @pl.when(me < peers - 1)
        def _():
            for g in range(count):
                link(g).wait_send()
            for g in range(count):
                to_peer(0, g).wait_recv()
                fin_ref[g * per_group : (g + 1) * per_group] = fin_recv[g]


def mix_kernel(
    x_ref, z_ref, b_ref, c_ref, skip_ref, gain_ref, ent_ref, shift_ref, last_ref, cols_ref,
    out_ref, state, parts, gated,
):
    groups, width, span = state.shape
    size = b_ref.shape[0]
    per_group = span // width

    @pl.when(pl.program_id(0) == 0)
    def _():
        for g in range(groups):
            for k in range(per_group):
                cols = slice(k * width, (k + 1) * width)
                entering = ent_ref[g, :, cols]
                high, low = split(entering)
                state[g, :, cols] = entering
                parts[g, :width, cols] = high
                parts[g, width:, cols] = low

    shift, last, cumul = shift_ref[0], last_ref[0], cols_ref[0]
    tails = jnp.exp2(last - shift)
    decays = jnp.exp2(last)
    rows = lax.broadcasted_iota(jnp.int32, (size, size), 0)
    cols_at = lax.broadcasted_iota(jnp.int32, (size, size), 1)
    causal = rows >= cols_at
    for g in range(groups):
        write = b_ref[:, g * width : (g + 1) * width]
        read = c_ref[:, g * width : (g + 1) * width]
        scores = lax.dot_general(
            read, write, (((1,), (1,)), ((), ())), preferred_element_type=F32
        )
        scores = jnp.where(causal, scores, 0.0)
        turned_b = jnp.transpose(write.astype(F32))
        earlier = jnp.dot(
            jnp.concatenate([read, read], axis=1), parts[g], preferred_element_type=F32
        )
        squares = jnp.zeros((size, width), F32)
        for k in range(per_group):
            h = g * per_group + k
            cols = slice(k * width, (k + 1) * width)
            wide = slice(h * width, (h + 1) * width)
            x = x_ref[:, wide]
            along = jnp.broadcast_to(cumul[:, h : h + 1], (size, width))
            weights = scores * jnp.exp2(jnp.minimum(along - shift[h : h + 1, :], 0.0))
            left = jnp.concatenate(
                [
                    jnp.concatenate(split(weights), axis=1),
                    jnp.concatenate(split(turned_b * tails[h : h + 1, :]), axis=1),
                ],
                axis=0,
            )
            both = jnp.dot(left, jnp.concatenate([x, x], axis=0), preferred_element_type=F32)
            later = decays[h : h + 1, :] * state[g, :, cols] + both[size:]
            high, low = split(later)
            state[g, :, cols] = later
            parts[g, :width, cols] = high
            parts[g, width:, cols] = low
            y = both[:size] + jnp.exp2(along) * earlier[:, cols] + skip_ref[h] * x.astype(F32)
            half = (0.5 * z_ref[:, wide]).astype(F32)
            value = y * half
            value = value + value * jnp.tanh(half)
            gated[:, cols] = value
            squares = squares + value * value
        mean = jnp.sum(squares, axis=1, keepdims=True) * (1.0 / span)
        scale = jnp.broadcast_to(lax.rsqrt(mean + 1e-05), (size, width))
        for k in range(per_group):
            h = g * per_group + k
            cols = slice(k * width, (k + 1) * width)
            wide = slice(h * width, (h + 1) * width)
            gain = gain_ref[pl.ds(h * width, width)].astype(F32).reshape(1, width)
            out_ref[:, wide] = (gated[:, cols] * scale * gain).astype(BF16)


def body(
    values, gate_in, write_proj, read_proj, step_size, log_gate, skip_gain, norm_gain, history
):
    heads, head_size, width = history.shape
    groups = write_proj.shape[1] // width
    per_group = heads // groups
    span = per_group * head_size
    rows = values.shape[0]
    peers = lax.axis_size("seq")
    share = head_size // peers
    size = math.gcd(rows, 128)
    blocks = rows // size
    big = math.gcd(rows, 512)

    def whole(*shape):
        return pl.BlockSpec(shape, lambda *_: (0,) * len(shape))

    entering, final_state, shifts, lasts, columns = pl.pallas_call(
        functools.partial(chain_kernel, peers),
        grid=(groups, rows // big),
        in_specs=[
            pl.BlockSpec((big, span), lambda g, c: (c, g)),
            pl.BlockSpec((big, width), lambda g, c: (c, g)),
            whole(heads, rows),
            whole(heads, rows),
            whole(heads, head_size, width),
        ],
        out_specs=[
            whole(groups, width, span),
            whole(heads, share, width),
            whole(blocks, heads, size),
            whole(blocks, heads, width),
            whole(blocks, size, heads),
        ],
        out_shape=[
            jax.ShapeDtypeStruct((groups, width, span), F32),
            jax.ShapeDtypeStruct((heads, share, width), F32),
            jax.ShapeDtypeStruct((blocks, heads, size), F32),
            jax.ShapeDtypeStruct((blocks, heads, width), F32),
            jax.ShapeDtypeStruct((blocks, size, heads), F32),
        ],
        scratch_shapes=[
            pltpu.VMEM((groups, width, span), F32),
            pltpu.VMEM((heads, width), F32),
            pltpu.VMEM((blocks, heads, size), F32),
            pltpu.VMEM((groups, width, span), F32),
            pltpu.VMEM((groups, width, span), F32),
            pltpu.VMEM((peers - 1, groups, per_group, share, width), F32),
            pltpu.VMEM((groups, per_group, share, width), F32),
            pltpu.SemaphoreType.DMA((groups,)),
            pltpu.SemaphoreType.DMA((groups,)),
            pltpu.SemaphoreType.DMA((peers - 1, groups)),
            pltpu.SemaphoreType.DMA((groups,)),
        ],
        compiler_params=pltpu.CompilerParams(
            collective_id=0, has_side_effects=True, vmem_limit_bytes=VMEM
        ),
        name="chain",
    )(values, write_proj, step_size.T, log_gate.T, history)

    normed = pl.pallas_call(
        mix_kernel,
        grid=(blocks,),
        in_specs=[
            pl.BlockSpec((size, heads * head_size), lambda c: (c, 0)),
            pl.BlockSpec((size, heads * head_size), lambda c: (c, 0)),
            pl.BlockSpec((size, groups * width), lambda c: (c, 0)),
            pl.BlockSpec((size, groups * width), lambda c: (c, 0)),
            pl.BlockSpec(memory_space=pltpu.SMEM),
            whole(heads * head_size),
            whole(groups, width, span),
            pl.BlockSpec((1, heads, size), lambda c: (c, 0, 0)),
            pl.BlockSpec((1, heads, width), lambda c: (c, 0, 0)),
            pl.BlockSpec((1, size, heads), lambda c: (c, 0, 0)),
        ],
        out_specs=pl.BlockSpec((size, heads * head_size), lambda c: (c, 0)),
        out_shape=jax.ShapeDtypeStruct((rows, heads * head_size), BF16),
        scratch_shapes=[
            pltpu.VMEM((groups, width, span), F32),
            pltpu.VMEM((groups, 2 * width, span), BF16),
            pltpu.VMEM((size, span), F32),
        ],
        compiler_params=pltpu.CompilerParams(vmem_limit_bytes=VMEM),
        name="mix",
    )(
        values, gate_in, write_proj, read_proj, skip_gain, norm_gain, entering,
        shifts, lasts, columns,
    )
    return normed, final_state


def solution(mesh):
    rows = P(("batch", "seq"), "tp")
    return jax.shard_map(
        body,
        mesh=mesh,
        in_specs=(rows, rows, rows, rows, rows, rows, P("tp"), P("tp"), P(("batch", "tp"), None, None)),
        out_specs=(rows, P(("batch", "tp"), "seq", None)),
        check_vma=False,
    )
```

```python
import functools
import math

import jax
import jax.numpy as jnp
from jax import lax
from jax.experimental import pallas as pl
from jax.experimental.pallas import tpu as pltpu
from jax.sharding import PartitionSpec as P

VMEM = 24 << 20
LOG2E = math.log2(math.e)
MESH = pl.DeviceIdType.MESH
F32 = jnp.float32
BF16 = jnp.bfloat16


def upper(size):
    rows = lax.broadcasted_iota(jnp.int32, (size, size), 0)
    cols = lax.broadcasted_iota(jnp.int32, (size, size), 1)
    return rows <= cols


def split(value):
    high = value.astype(BF16)
    low = (value - high.astype(F32)).astype(BF16)
    return high, low


def prefix_sums(rows):
    size = rows.shape[1]
    first = rows.astype(BF16)
    rest = rows - first.astype(F32)
    second = rest.astype(BF16)
    third = (rest - second.astype(F32)).astype(BF16)
    ones = upper(size).astype(BF16)
    return jnp.dot(
        jnp.concatenate([first, second, third], axis=1),
        jnp.concatenate([ones, ones, ones], axis=0),
        preferred_element_type=F32,
    )


def chain_kernel(
    peers, x_hbm, z_hbm, b_hbm, c_hbm, step_hbm, gate_hbm, hist_hbm, skip_hbm,
    fin_ref, ent_ref, delta_ref, y_ref, z_ref, c_ref, cols_ref, decay_ref,
    x_ref, b_ref, step_ref, gate_ref, hist_ref, skip_ref, shift_ref, tail_ref,
    state, total, recv, send, full, fin_recv,
    x_sem, z_sem, c_sem, b_sem, load_sem, send_sem, recv_sem, fin_send_sem, fin_recv_sem,
):
    count, width, span = recv.shape
    blocks, heads, size = shift_ref.shape
    me = lax.axis_index("seq")
    per_group = heads // count
    share = fin_ref.shape[1]

    def peer(d):
        return dict(device_id={"seq": d}, device_id_type=MESH)

    barrier = pltpu.get_barrier_semaphore()
    for by in range(1, peers):
        pl.semaphore_signal(barrier, inc=1, **peer(lax.rem(me + by, peers)))

    def block_copy(source, target, sem, c):
        return pltpu.make_async_copy(source.at[pl.ds(c * size, size)], target.at[c], sem.at[c])

    small = [
        pltpu.make_async_copy(gate_hbm, gate_ref, load_sem.at[0]),
        pltpu.make_async_copy(step_hbm, step_ref, load_sem.at[1]),
        pltpu.make_async_copy(hist_hbm, hist_ref, load_sem.at[2]),
        pltpu.make_async_copy(skip_hbm, skip_ref, load_sem.at[3]),
    ]
    small[0].start()
    small[1].start()
    for c in range(blocks):
        block_copy(b_hbm, b_ref, b_sem, c).start()
        block_copy(x_hbm, x_ref, x_sem, c).start()
    small[2].start()
    small[3].start()
    for c in range(blocks):
        block_copy(c_hbm, c_ref, c_sem, c).start()
    for c in range(blocks):
        block_copy(z_hbm, z_ref, z_sem, c).start()
    small[0].wait()
    small[1].wait()

    rows = [gate_ref[:, c * size : (c + 1) * size] for c in range(blocks)]
    cumul = prefix_sums(jnp.concatenate(rows, axis=0) * LOG2E)
    columns = jnp.transpose(cumul)
    after = jnp.zeros((heads, width), F32)
    for c in range(blocks):
        here = cumul[c * heads : (c + 1) * heads]
        shift = here - jnp.log2(step_ref[:, c * size : (c + 1) * size])
        last = jnp.broadcast_to(here[:, size - 1 : size], (heads, width))
        shift_ref[c] = shift
        cols_ref[c] = columns[:, c * heads : (c + 1) * heads]
        decay_ref[c] = jnp.exp2(last)
        tail_ref[c] = jnp.exp2(last - shift)
        after = after + last
    total[...] = jnp.exp2(after)
    state[...] = jnp.zeros_like(state)

    def gather(c, carry):
        block_copy(b_hbm, b_ref, b_sem, c).wait()
        block_copy(x_hbm, x_ref, x_sem, c).wait()
        tails, decays = tail_ref[c], decay_ref[c]
        for g in range(count):
            turned_b = jnp.transpose(b_ref[c, :, g * width : (g + 1) * width].astype(F32))
            for k in range(per_group):
                h = g * per_group + k
                cols = slice(k * width, (k + 1) * width)
                x = x_ref[c, :, h * width : (h + 1) * width]
                left = jnp.concatenate(split(turned_b * tails[h : h + 1, :]), axis=1)
                delta = jnp.dot(
                    left, jnp.concatenate([x, x], axis=0), preferred_element_type=F32
                )
                delta_ref[c, g, :, cols] = delta
                state[g, :, cols] = decays[h : h + 1, :] * state[g, :, cols] + delta
        return carry

    lax.fori_loop(0, blocks, gather, 0)

    def link(g):
        return pltpu.make_async_remote_copy(
            src_ref=send.at[g], dst_ref=recv.at[g],
            send_sem=send_sem.at[g], recv_sem=recv_sem.at[g],
            **peer(jnp.minimum(me + 1, peers - 1)),
        )

    def to_peer(d, g):
        return pltpu.make_async_remote_copy(
            src_ref=full.at[d, g], dst_ref=fin_recv.at[g],
            send_sem=fin_send_sem.at[d, g], recv_sem=fin_recv_sem.at[g],
            **peer(d),
        )

    def enter(g, k, entering):
        h = g * per_group + k
        cols = slice(k * width, (k + 1) * width)
        ent_ref[g, :, cols] = entering
        send[g, :, cols] = total[h : h + 1, :] * entering + state[g, :, cols]

    small[2].wait()
    small[3].wait()
    pl.semaphore_wait(barrier, peers - 1)

    @pl.when(me == 0)
    def _():
        for g in range(count):
            for k in range(per_group):
                enter(g, k, jnp.transpose(hist_ref[g * per_group + k]))
            link(g).start()

    causal = lax.broadcasted_iota(jnp.int32, (size, size), 0) >= lax.broadcasted_iota(
        jnp.int32, (size, size), 1
    )

    def within(c, carry):
        block_copy(c_hbm, c_ref, c_sem, c).wait()
        shift, cumul = shift_ref[c], cols_ref[c]
        for g in range(count):
            scores = lax.dot_general(
                c_ref[c, :, g * width : (g + 1) * width],
                b_ref[c, :, g * width : (g + 1) * width],
                (((1,), (1,)), ((), ())),
                preferred_element_type=F32,
            )
            scores = jnp.where(causal, scores, 0.0)
            for k in range(per_group):
                h = g * per_group + k
                wide = slice(h * width, (h + 1) * width)
                x = x_ref[c, :, wide]
                along = jnp.broadcast_to(cumul[:, h : h + 1], (size, size))
                weights = scores * jnp.exp2(jnp.minimum(along - shift[h : h + 1, :], 0.0))
                y_ref[c, :, wide] = skip_ref[h] * x.astype(F32) + jnp.dot(
                    jnp.concatenate(split(weights), axis=1),
                    jnp.concatenate([x, x], axis=0),
                    preferred_element_type=F32,
                )
        return carry

    middle = (blocks + 1) // 2
    lax.fori_loop(0, middle, within, 0)

    @pl.when(me > 0)
    def _():
        for g in range(count):
            link(g).wait_recv()
            for k in range(per_group):
                enter(g, k, recv[g, :, k * width : (k + 1) * width])

            @pl.when(me < peers - 1)
            def _(g=g):
                link(g).start()

            @pl.when(me == peers - 1)
            def _(g=g):
                for k in range(per_group):
                    closing = jnp.transpose(send[g, :, k * width : (k + 1) * width])
                    for d in range(peers - 1):
                        full[d, g, k] = closing[d * share : (d + 1) * share]
                    fin_ref[g * per_group + k] = closing[(peers - 1) * share :]
                for d in range(peers - 1):
                    to_peer(d, g).start()

    lax.fori_loop(middle, blocks, within, 0)
    for c in range(blocks):
        block_copy(z_hbm, z_ref, z_sem, c).wait()

    @pl.when(me == peers - 1)
    def _():
        for g in range(count):
            for d in range(peers - 1):
                to_peer(d, g).wait_send()

    @pl.when(me < peers - 1)
    def _():
        for g in range(count):
            link(g).wait_send()
        for g in range(count):
            to_peer(0, g).wait_recv()
            fin_ref[g * per_group : (g + 1) * per_group] = fin_recv[g]


def mix_kernel(
    gain_ref, ent_ref, delta_ref, y_ref, z_ref, c_ref, cols_ref, decay_ref,
    out_hbm, state, parts, gated, out_ref, out_sem,
):
    groups, width, span = state.shape
    blocks, size = c_ref.shape[:2]
    per_group = span // width

    for g in range(groups):
        for k in range(per_group):
            cols = slice(k * width, (k + 1) * width)
            entering = ent_ref[g, :, cols]
            high, low = split(entering)
            state[g, :, cols] = entering
            parts[g, :width, cols] = high
            parts[g, width:, cols] = low

    def out_copy(c):
        return pltpu.make_async_copy(
            out_ref.at[c], out_hbm.at[pl.ds(c * size, size)], out_sem.at[c]
        )

    def block(c, carry):
        cumul, decays = cols_ref[c], decay_ref[c]
        for g in range(groups):
            read = c_ref[c, :, g * width : (g + 1) * width]
            earlier = jnp.dot(
                jnp.concatenate([read, read], axis=1), parts[g], preferred_element_type=F32
            )
            squares = jnp.zeros((size, width), F32)
            for k in range(per_group):
                h = g * per_group + k
                cols = slice(k * width, (k + 1) * width)
                wide = slice(h * width, (h + 1) * width)
                later = decays[h : h + 1, :] * state[g, :, cols] + delta_ref[c, g, :, cols]
                high, low = split(later)
                state[g, :, cols] = later
                parts[g, :width, cols] = high
                parts[g, width:, cols] = low
                along = jnp.broadcast_to(cumul[:, h : h + 1], (size, width))
                y = y_ref[c, :, wide] + jnp.exp2(along) * earlier[:, cols]
                half = (0.5 * z_ref[c, :, wide]).astype(F32)
                value = y * half
                value = value + value * jnp.tanh(half)
                gated[:, cols] = value
                squares = squares + value * value
            mean = jnp.sum(squares, axis=1, keepdims=True) * (1.0 / span)
            scale = jnp.broadcast_to(lax.rsqrt(mean + 1e-05), (size, width))
            for k in range(per_group):
                h = g * per_group + k
                cols = slice(k * width, (k + 1) * width)
                wide = slice(h * width, (h + 1) * width)
                gain = gain_ref[pl.ds(h * width, width)].astype(F32).reshape(1, width)
                out_ref[c, :, wide] = (gated[:, cols] * scale * gain).astype(BF16)
        out_copy(c).start()
        return carry

    lax.fori_loop(0, blocks, block, 0)
    for c in range(blocks):
        out_copy(c).wait()


def body(
    values, gate_in, write_proj, read_proj, step_size, log_gate, skip_gain, norm_gain, history
):
    heads, head_size, width = history.shape
    groups = write_proj.shape[1] // width
    per_group = heads // groups
    span = per_group * head_size
    rows = values.shape[0]
    peers = lax.axis_size("seq")
    share = head_size // peers
    size = math.gcd(rows, 128)
    blocks = rows // size
    size = math.gcd(rows, 128)
    blocks = rows // size
    in_vmem = pl.BlockSpec(memory_space=pltpu.VMEM)
    in_hbm = pl.BlockSpec(memory_space=pltpu.HBM)
    dma = pltpu.SemaphoreType.DMA

    final_state, *handed = pl.pallas_call(
        functools.partial(chain_kernel, peers),
        in_specs=[in_hbm] * 8,
        out_specs=[in_vmem] * 8,
        out_shape=[
            jax.ShapeDtypeStruct((heads, share, width), F32),
            pltpu.VMEM((groups, width, span), F32),
            pltpu.VMEM((blocks, groups, width, span), F32),
            pltpu.VMEM((blocks, size, heads * head_size), F32),
            pltpu.VMEM((blocks, size, heads * head_size), BF16),
            pltpu.VMEM((blocks, size, groups * width), BF16),
            pltpu.VMEM((blocks, size, heads), F32),
            pltpu.VMEM((blocks, heads, width), F32),
        ],
        scratch_shapes=[
            pltpu.VMEM((blocks, size, heads * head_size), BF16),
            pltpu.VMEM((blocks, size, groups * width), BF16),
            pltpu.VMEM((heads, rows), F32),
            pltpu.VMEM((heads, rows), F32),
            pltpu.VMEM((heads, head_size, width), F32),
            pltpu.SMEM((heads,), F32),
            pltpu.VMEM((blocks, heads, size), F32),
            pltpu.VMEM((blocks, heads, size), F32),
            pltpu.VMEM((groups, width, span), F32),
            pltpu.VMEM((heads, width), F32),
            pltpu.VMEM((groups, width, span), F32),
            pltpu.VMEM((groups, width, span), F32),
            pltpu.VMEM((peers - 1, groups, per_group, share, width), F32),
            pltpu.VMEM((groups, per_group, share, width), F32),
            dma((blocks,)),
            dma((blocks,)),
            dma((blocks,)),
            dma((blocks,)),
            dma((4,)),
            dma((groups,)),
            dma((groups,)),
            dma((peers - 1, groups)),
            dma((groups,)),
        ],
        compiler_params=pltpu.CompilerParams(
            collective_id=0, has_side_effects=True, vmem_limit_bytes=VMEM
        ),
        name="chain",
    )(
        *(
            pltpu.with_memory_space_constraint(array, pltpu.HBM)
            for array in (
                values, gate_in, write_proj, read_proj, step_size.T, log_gate.T, history,
                skip_gain,
            )
        )
    )

    normed = pl.pallas_call(
        mix_kernel,
        in_specs=[in_vmem] * 8,
        out_specs=in_hbm,
        out_shape=jax.ShapeDtypeStruct((rows, heads * head_size), BF16),
        scratch_shapes=[
            pltpu.VMEM((groups, width, span), F32),
            pltpu.VMEM((groups, 2 * width, span), BF16),
            pltpu.VMEM((size, span), F32),
            pltpu.VMEM((blocks, size, heads * head_size), BF16),
            dma((blocks,)),
        ],
        compiler_params=pltpu.CompilerParams(vmem_limit_bytes=VMEM),
        name="mix",
    )(norm_gain, *handed)
    return normed, final_state


def solution(mesh):
    rows = P(("batch", "seq"), "tp")
    return jax.shard_map(
        body,
        mesh=mesh,
        in_specs=(rows, rows, rows, rows, rows, rows, P("tp"), P("tp"), P(("batch", "tp"), None, None)),
        out_specs=(rows, P(("batch", "tp"), "seq", None)),
        check_vma=False,
    )
```

```python
import functools
import math

import jax
import jax.numpy as jnp
from jax import lax
from jax.experimental import pallas as pl
from jax.experimental.pallas import tpu as pltpu
from jax.sharding import PartitionSpec as P

VMEM = 24 << 20
LOG2E = math.log2(math.e)
MESH = pl.DeviceIdType.MESH
F32 = jnp.float32
BF16 = jnp.bfloat16


def upper(size):
    rows = lax.broadcasted_iota(jnp.int32, (size, size), 0)
    cols = lax.broadcasted_iota(jnp.int32, (size, size), 1)
    return rows <= cols


def split(value):
    high = value.astype(BF16)
    low = (value - high.astype(F32)).astype(BF16)
    return high, low


def prefix_sums(rows):
    size = rows.shape[1]
    first = rows.astype(BF16)
    rest = rows - first.astype(F32)
    second = rest.astype(BF16)
    third = (rest - second.astype(F32)).astype(BF16)
    ones = upper(size).astype(BF16)
    return jnp.dot(
        jnp.concatenate([first, second, third], axis=1),
        jnp.concatenate([ones, ones, ones], axis=0),
        preferred_element_type=F32,
    )


def chain_kernel(
    peers, x_hbm, z_hbm, b_hbm, c_hbm, step_hbm, gate_hbm, hist_hbm, skip_hbm,
    fin_ref, ent_ref, delta_ref, y_ref, z_ref, c_ref, cols_ref, decay_ref,
    x_ref, b_ref, step_ref, gate_ref, hist_ref, skip_ref, shift_ref, tail_ref,
    state, total, recv, send, full, fin_recv,
    x_sem, z_sem, c_sem, b_sem, load_sem, send_sem, recv_sem, fin_send_sem, fin_recv_sem,
):
    count, width, span = recv.shape
    blocks, heads, size = shift_ref.shape
    me = lax.axis_index("seq")
    per_group = heads // count
    share = fin_ref.shape[1]

    def peer(d):
        return dict(device_id={"seq": d}, device_id_type=MESH)

    barrier = pltpu.get_barrier_semaphore()
    for by in range(1, peers):
        pl.semaphore_signal(barrier, inc=1, **peer(lax.rem(me + by, peers)))

    def block_copy(source, target, sem, c):
        return pltpu.make_async_copy(source.at[pl.ds(c * size, size)], target.at[c], sem.at[c])

    small = [
        pltpu.make_async_copy(gate_hbm, gate_ref, load_sem.at[0]),
        pltpu.make_async_copy(step_hbm, step_ref, load_sem.at[1]),
        pltpu.make_async_copy(hist_hbm, hist_ref, load_sem.at[2]),
        pltpu.make_async_copy(skip_hbm, skip_ref, load_sem.at[3]),
    ]
    small[0].start()
    small[1].start()
    for c in range(blocks):
        block_copy(b_hbm, b_ref, b_sem, c).start()
        block_copy(x_hbm, x_ref, x_sem, c).start()
    small[2].start()
    small[3].start()
    for c in range(blocks):
        block_copy(c_hbm, c_ref, c_sem, c).start()
    for c in range(blocks):
        block_copy(z_hbm, z_ref, z_sem, c).start()
    small[0].wait()
    small[1].wait()

    rows = [gate_ref[:, c * size : (c + 1) * size] for c in range(blocks)]
    cumul = prefix_sums(jnp.concatenate(rows, axis=0) * LOG2E)
    columns = jnp.transpose(cumul)
    after = jnp.zeros((heads, width), F32)
    for c in range(blocks):
        here = cumul[c * heads : (c + 1) * heads]
        shift = here - jnp.log2(step_ref[:, c * size : (c + 1) * size])
        last = jnp.broadcast_to(here[:, size - 1 : size], (heads, width))
        shift_ref[c] = shift
        cols_ref[c] = columns[:, c * heads : (c + 1) * heads]
        decay_ref[c] = jnp.exp2(last)
        tail_ref[c] = jnp.exp2(last - shift)
        after = after + last
    total[...] = jnp.exp2(after)
    state[...] = jnp.zeros_like(state)

    def gather(c, carry):
        block_copy(b_hbm, b_ref, b_sem, c).wait()
        block_copy(x_hbm, x_ref, x_sem, c).wait()
        tails, decays = tail_ref[c], decay_ref[c]
        for g in range(count):
            turned_b = jnp.transpose(b_ref[c, :, g * width : (g + 1) * width].astype(F32))
            for k in range(per_group):
                h = g * per_group + k
                cols = slice(k * width, (k + 1) * width)
                x = x_ref[c, :, h * width : (h + 1) * width]
                left = jnp.concatenate(split(turned_b * tails[h : h + 1, :]), axis=1)
                delta = jnp.dot(
                    left, jnp.concatenate([x, x], axis=0), preferred_element_type=F32
                )
                delta_ref[c, g, :, cols] = delta
                state[g, :, cols] = decays[h : h + 1, :] * state[g, :, cols] + delta
        return carry

    lax.fori_loop(0, blocks, gather, 0)

    def link(g):
        return pltpu.make_async_remote_copy(
            src_ref=send.at[g], dst_ref=recv.at[g],
            send_sem=send_sem.at[g], recv_sem=recv_sem.at[g],
            **peer(jnp.minimum(me + 1, peers - 1)),
        )

    def to_peer(d, g):
        return pltpu.make_async_remote_copy(
            src_ref=full.at[d, g], dst_ref=fin_recv.at[g],
            send_sem=fin_send_sem.at[d, g], recv_sem=fin_recv_sem.at[g],
            **peer(d),
        )

    def enter(g, k, entering):
        h = g * per_group + k
        cols = slice(k * width, (k + 1) * width)
        ent_ref[g, :, cols] = entering
        send[g, :, cols] = total[h : h + 1, :] * entering + state[g, :, cols]

    small[2].wait()
    small[3].wait()
    pl.semaphore_wait(barrier, peers - 1)

    @pl.when(me == 0)
    def _():
        for g in range(count):
            for k in range(per_group):
                enter(g, k, jnp.transpose(hist_ref[g * per_group + k]))
            link(g).start()

    causal = lax.broadcasted_iota(jnp.int32, (size, size), 0) >= lax.broadcasted_iota(
        jnp.int32, (size, size), 1
    )

    def within(c, carry):
        block_copy(c_hbm, c_ref, c_sem, c).wait()
        shift, cumul = shift_ref[c], cols_ref[c]
        for g in range(count):
            scores = lax.dot_general(
                c_ref[c, :, g * width : (g + 1) * width],
                b_ref[c, :, g * width : (g + 1) * width],
                (((1,), (1,)), ((), ())),
                preferred_element_type=F32,
            )
            scores = jnp.where(causal, scores, 0.0)
            for k in range(per_group):
                h = g * per_group + k
                wide = slice(h * width, (h + 1) * width)
                x = x_ref[c, :, wide]
                along = jnp.broadcast_to(cumul[:, h : h + 1], (size, size))
                weights = scores * jnp.exp2(jnp.minimum(along - shift[h : h + 1, :], 0.0))
                y_ref[c, :, wide] = skip_ref[h] * x.astype(F32) + jnp.dot(
                    jnp.concatenate(split(weights), axis=1),
                    jnp.concatenate([x, x], axis=0),
                    preferred_element_type=F32,
                )
        return carry

    middle = (blocks + 1) // 2
    lax.fori_loop(0, middle, within, 0)

    @pl.when(me > 0)
    def _():
        for g in range(count):
            link(g).wait_recv()
            for k in range(per_group):
                enter(g, k, recv[g, :, k * width : (k + 1) * width])

            @pl.when(me < peers - 1)
            def _(g=g):
                link(g).start()

            @pl.when(me == peers - 1)
            def _(g=g):
                for k in range(per_group):
                    closing = jnp.transpose(send[g, :, k * width : (k + 1) * width])
                    for d in range(peers - 1):
                        full[d, g, k] = closing[d * share : (d + 1) * share]
                    fin_ref[g * per_group + k] = closing[(peers - 1) * share :]
                for d in range(peers - 1):
                    to_peer(d, g).start()

    lax.fori_loop(middle, blocks, within, 0)
    for c in range(blocks):
        block_copy(z_hbm, z_ref, z_sem, c).wait()

    @pl.when(me == peers - 1)
    def _():
        for g in range(count):
            for d in range(peers - 1):
                to_peer(d, g).wait_send()

    @pl.when(me < peers - 1)
    def _():
        for g in range(count):
            link(g).wait_send()
        for g in range(count):
            to_peer(0, g).wait_recv()
            fin_ref[g * per_group : (g + 1) * per_group] = fin_recv[g]


def mix_kernel(
    gain_ref, ent_ref, delta_ref, y_ref, z_ref, c_ref, cols_ref, decay_ref,
    out_hbm, state, parts, gated, out_ref, out_sem,
):
    groups, width, span = state.shape
    blocks, size = c_ref.shape[:2]
    per_group = span // width

    for g in range(groups):
        for k in range(per_group):
            cols = slice(k * width, (k + 1) * width)
            entering = ent_ref[g, :, cols]
            high, low = split(entering)
            state[g, :, cols] = entering
            parts[g, :width, cols] = high
            parts[g, width:, cols] = low

    def out_copy(c):
        return pltpu.make_async_copy(
            out_ref.at[c], out_hbm.at[pl.ds(c * size, size)], out_sem.at[c]
        )

    def block(c, carry):
        cumul, decays = cols_ref[c], decay_ref[c]
        for g in range(groups):
            read = c_ref[c, :, g * width : (g + 1) * width]
            earlier = jnp.dot(
                jnp.concatenate([read, read], axis=1), parts[g], preferred_element_type=F32
            )
            squares = jnp.zeros((size, width), F32)
            for k in range(per_group):
                h = g * per_group + k
                cols = slice(k * width, (k + 1) * width)
                wide = slice(h * width, (h + 1) * width)
                later = decays[h : h + 1, :] * state[g, :, cols] + delta_ref[c, g, :, cols]
                high, low = split(later)
                state[g, :, cols] = later
                parts[g, :width, cols] = high
                parts[g, width:, cols] = low
                along = jnp.broadcast_to(cumul[:, h : h + 1], (size, width))
                y = y_ref[c, :, wide] + jnp.exp2(along) * earlier[:, cols]
                half = (0.5 * z_ref[c, :, wide]).astype(F32)
                value = y * half
                value = value + value * jnp.tanh(half)
                gated[:, cols] = value
                squares = squares + value * value
            mean = jnp.sum(squares, axis=1, keepdims=True) * (1.0 / span)
            scale = jnp.broadcast_to(lax.rsqrt(mean + 1e-05), (size, width))
            for k in range(per_group):
                h = g * per_group + k
                cols = slice(k * width, (k + 1) * width)
                wide = slice(h * width, (h + 1) * width)
                gain = gain_ref[pl.ds(h * width, width)].astype(F32).reshape(1, width)
                out_ref[c, :, wide] = (gated[:, cols] * scale * gain).astype(BF16)
        out_copy(c).start()
        return carry

    lax.fori_loop(0, blocks, block, 0, unroll=2 if blocks % 2 == 0 else 1)
    for c in range(blocks):
        out_copy(c).wait()


def body(
    values, gate_in, write_proj, read_proj, step_size, log_gate, skip_gain, norm_gain, history
):
    heads, head_size, width = history.shape
    groups = write_proj.shape[1] // width
    per_group = heads // groups
    span = per_group * head_size
    rows = values.shape[0]
    peers = lax.axis_size("seq")
    share = head_size // peers
    size = math.gcd(rows, 128)
    blocks = rows // size
    size = math.gcd(rows, 128)
    blocks = rows // size
    in_vmem = pl.BlockSpec(memory_space=pltpu.VMEM)
    in_hbm = pl.BlockSpec(memory_space=pltpu.HBM)
    dma = pltpu.SemaphoreType.DMA

    final_state, *handed = pl.pallas_call(
        functools.partial(chain_kernel, peers),
        in_specs=[in_hbm] * 8,
        out_specs=[in_vmem] * 8,
        out_shape=[
            jax.ShapeDtypeStruct((heads, share, width), F32),
            pltpu.VMEM((groups, width, span), F32),
            pltpu.VMEM((blocks, groups, width, span), F32),
            pltpu.VMEM((blocks, size, heads * head_size), F32),
            pltpu.VMEM((blocks, size, heads * head_size), BF16),
            pltpu.VMEM((blocks, size, groups * width), BF16),
            pltpu.VMEM((blocks, size, heads), F32),
            pltpu.VMEM((blocks, heads, width), F32),
        ],
        scratch_shapes=[
            pltpu.VMEM((blocks, size, heads * head_size), BF16),
            pltpu.VMEM((blocks, size, groups * width), BF16),
            pltpu.VMEM((heads, rows), F32),
            pltpu.VMEM((heads, rows), F32),
            pltpu.VMEM((heads, head_size, width), F32),
            pltpu.SMEM((heads,), F32),
            pltpu.VMEM((blocks, heads, size), F32),
            pltpu.VMEM((blocks, heads, size), F32),
            pltpu.VMEM((groups, width, span), F32),
            pltpu.VMEM((heads, width), F32),
            pltpu.VMEM((groups, width, span), F32),
            pltpu.VMEM((groups, width, span), F32),
            pltpu.VMEM((peers - 1, groups, per_group, share, width), F32),
            pltpu.VMEM((groups, per_group, share, width), F32),
            dma((blocks,)),
            dma((blocks,)),
            dma((blocks,)),
            dma((blocks,)),
            dma((4,)),
            dma((groups,)),
            dma((groups,)),
            dma((peers - 1, groups)),
            dma((groups,)),
        ],
        compiler_params=pltpu.CompilerParams(
            collective_id=0, has_side_effects=True, vmem_limit_bytes=VMEM
        ),
        name="chain",
    )(
        *(
            pltpu.with_memory_space_constraint(array, pltpu.HBM)
            for array in (
                values, gate_in, write_proj, read_proj, step_size.T, log_gate.T, history,
                skip_gain,
            )
        )
    )

    normed = pl.pallas_call(
        mix_kernel,
        in_specs=[in_vmem] * 8,
        out_specs=in_hbm,
        out_shape=jax.ShapeDtypeStruct((rows, heads * head_size), BF16),
        scratch_shapes=[
            pltpu.VMEM((groups, width, span), F32),
            pltpu.VMEM((groups, 2 * width, span), BF16),
            pltpu.VMEM((size, span), F32),
            pltpu.VMEM((blocks, size, heads * head_size), BF16),
            dma((blocks,)),
        ],
        compiler_params=pltpu.CompilerParams(vmem_limit_bytes=VMEM),
        name="mix",
    )(norm_gain, *handed)
    return normed, final_state


def solution(mesh):
    rows = P(("batch", "seq"), "tp")
    return jax.shard_map(
        body,
        mesh=mesh,
        in_specs=(rows, rows, rows, rows, rows, rows, P("tp"), P("tp"), P(("batch", "tp"), None, None)),
        out_specs=(rows, P(("batch", "tp"), "seq", None)),
        check_vma=False,
    )
```
